32 devices in a mesh: group: 2 (over x), row: 8 (over z, y), rhs: 2 (over core).
Axes of the slice: x: 2, y: 2, z: 4, core: 2. Of those that a mesh axis runs over, the one named last changes fastest.
Arguments:
- u_panels: float32 [8192, 1536], P(('group', 'row')), parts along dimension 0, may hold values from -0.078125 to 0.078125
- u_diag: float32 [3072], P('group'), parts along dimension 0, may hold values from 0.5 to 2
- l_panels: float32 [8192, 1536], P(('group', 'row')), parts along dimension 0, may hold values from -0.078125 to 0.078125
- right_side: float32 [8192, 512], P(('group', 'row'), 'rhs'), parts along dimension 0, may hold values from -6 to 6
- x_tail: float32 [8192, 512], P(('group', 'row'), 'rhs'), parts along dimension 0, may hold values from -6 to 6
- slot_blocks: int32 [16], P('group'), parts along dimension 0, may hold values from 0 to 7, as said below
Outputs:
- forward_out: float32 [8192, 512], P(('group', 'row'), 'rhs'), parts along dimension 0
- solution: float32 [8192, 512], P(('group', 'row'), 'rhs'), parts along dimension 0
The draws below stay inside these ranges and needn't reach their ends.
There are 2 independent parts, one for each index of `group`. The reference program is written for one: setup_inputs(seed, part) draws one part's arguments, and reference() takes and returns one part's arrays. A program takes and returns all parts, laid end to end along the dimension named above; each array names one. Nothing has to cross between parts.
Inputs may be any that keep to these rules, and one draw needn't show every extreme that they name: `slot_blocks`: a permutation of the 8 global row blocks, each named once.
All inputs are finite; a program needn't handle non-finite values.
Results may differ from the reference program's by a relative error of at most 0.000065.
Values sent between devices are 32-bit elements; how exact they have to be, the bound alone decides.
No kernel may reach another device: no remote copies, remote signals or barrier semaphores. Data moves between devices by JAX's collectives and lax.ppermute only.
A program may use at most 64 MiB of HBM per device.

```python
import math
import jax
import jax.numpy as jnp
from jax import lax

PANEL = 512
PANELS = 3
BLOCKS = 8
RHS = 512


def draw_slot_blocks(key, part):
    return jax.random.permutation(key, BLOCKS).astype(jnp.int32)


def shard_levels(stream_key, shape, shards, low, largest):
    loudness, own = 1.0, jax.random.fold_in(stream_key, 6)
    for dim, blocks in shards:
        steps = jnp.exp(jax.random.uniform(jax.random.fold_in(own, dim), (blocks,), jnp.float32, low / len(shards), largest / len(shards)))
        loudness = loudness * jnp.repeat(steps, shape[dim] // blocks).reshape([-1 if axis == dim else 1 for axis in range(len(shape))])
    return loudness


def gaussian(own_key, dims, width, most, pieces=(), held_as=jnp.bfloat16):
    values = width * jax.random.normal(own_key, dims, jnp.float32)
    if pieces:
        values = values * shard_levels(own_key, dims, pieces, -0.22, 0.18)
    return jnp.clip(values, -most, most).astype(held_as)


def setup_inputs(seed: int = 0, part: int = 0) -> dict:
    key_list = jax.random.split(jax.random.key(seed), 7)
    own_keys = jax.random.split(jax.random.fold_in(key_list[6], part), 7)
    return {
        "u_panels": gaussian(own_keys[0], (BLOCKS * PANEL, PANELS * PANEL), (4 * PANELS * PANEL) ** -0.5, 0.078125, ((0, 8),), jnp.float32),
        "u_diag": jnp.clip(jnp.exp(jax.random.uniform(own_keys[1], (PANELS * PANEL,), jnp.float32, math.log(0.5), math.log(2.0))), 0.5, 2.0),
        "l_panels": gaussian(own_keys[2], (BLOCKS * PANEL, PANELS * PANEL), (4 * PANELS * PANEL) ** -0.5, 0.078125, ((0, 8),), jnp.float32),
        "right_side": gaussian(own_keys[3], (BLOCKS * PANEL, RHS), 1.0, 6.0, ((0, 8), (1, 2)), jnp.float32),
        "x_tail": gaussian(own_keys[4], (BLOCKS * PANEL, RHS), 1.0, 6.0, ((0, 8), (1, 2)), jnp.float32),
        "slot_blocks": draw_slot_blocks(jax.random.fold_in(jax.random.fold_in(key_list[6], part), 71), part),
    }


def to_global(stored, slot_blocks):
    shaped = stored.reshape((BLOCKS, PANEL) + stored.shape[1:])
    placed = jnp.zeros_like(shaped).at[slot_blocks].set(shaped)
    return placed.reshape(stored.shape)

def to_stored(whole, slot_blocks):
    shaped = whole.reshape((BLOCKS, PANEL) + whole.shape[1:])
    return shaped[slot_blocks].reshape(whole.shape)

def reference(u_panels, u_diag, l_panels, right_side, x_tail, slot_blocks):
    head = PANELS * PANEL
    total_rows = BLOCKS * PANEL
    row_ids = lax.broadcasted_iota(jnp.int32, (total_rows, head), 0)
    col_ids = lax.broadcasted_iota(jnp.int32, (total_rows, head), 1)
    strict = row_ids > col_ids
    upper_low = jnp.where(strict, to_global(u_panels, slot_blocks), 0.0)
    lower_low = jnp.where(strict, to_global(l_panels, slot_blocks), 0.0)
    rhs_global = to_global(right_side, slot_blocks)
    tail_global = to_global(x_tail, slot_blocks)
    head_upper = upper_low[:head] + jnp.diag(u_diag)
    forward_head = lax.linalg.triangular_solve(head_upper, rhs_global[:head], left_side=True, lower=True)
    forward_tail = rhs_global[head:] - jnp.dot(upper_low[head:].astype(jnp.float32), forward_head.astype(jnp.float32), precision=lax.Precision.HIGHEST, preferred_element_type=jnp.float32)
    forward_all = jnp.concatenate([forward_head, forward_tail], axis=0)
    coupled = lax.dot_general(lower_low[head:].astype(jnp.float32), tail_global[head:].astype(jnp.float32), (((0,), (0,)), ((), ())), precision=lax.Precision.HIGHEST, preferred_element_type=jnp.float32)
    solution_head = lax.linalg.triangular_solve(lower_low[:head], forward_head - coupled, left_side=True, lower=True, transpose_a=True, unit_diagonal=True)
    solution_all = jnp.concatenate([solution_head, tail_global[head:]], axis=0)
    return (to_stored(forward_all, slot_blocks), to_stored(solution_all, slot_blocks))
```

```python
import functools

import jax
import jax.numpy as jnp
from jax import lax
from jax.experimental import pallas as pl
from jax.experimental.pallas import tpu as pltpu
from jax.sharding import PartitionSpec as P

PANEL = 512
PANELS = 3
CHUNKS = 2
BASE = 8
STRIP = 128
F32 = jnp.float32
BF16 = jnp.bfloat16


def split(value):
    high = value.astype(BF16)
    return high, (value - high.astype(F32)).astype(BF16)


def single(left, right):
    return jnp.dot(left, right, preferred_element_type=F32)


def times(left, right):
    return single(left[0], right[0]) + (single(left[0], right[1]) + single(left[1], right[0]))


def unit_inverses(strict, size):
    row = lax.broadcasted_iota(jnp.int32, (size, size), 0)
    col = lax.broadcasted_iota(jnp.int32, (size, size), 1)
    eye = jnp.where(row == col, 1.0, 0.0)
    powers = [jnp.where(row // BASE == col // BASE, -m, 0.0) for m in strict]
    inverses = [eye + p for p in powers]
    reach = 2
    while reach < BASE:
        halves = [split(p) for p in powers]
        powers = [times(h, h) for h in halves]
        inverses = [x + times(split(p), split(x)) for x, p in zip(inverses, powers)]
        reach *= 2
    block = BASE
    while block < size:
        pair = (row // (2 * block) == col // (2 * block)) & (row // block > col // block)
        between = [split(jnp.where(pair, m, 0.0)) for m in strict]
        halves = [split(x) for x in inverses]
        moved = [times(o, h) for o, h in zip(between, halves)]
        inverses = [x - times(h, split(t)) for x, h, t in zip(inverses, halves, moved)]
        block *= 2
    return inverses


def inverse_kernel(panel_ref, u_ref, l_ref, diag_row_ref, diag_col_ref, u_out, l_out):
    size = u_ref.shape[0]
    row = lax.broadcasted_iota(jnp.int32, (STRIP, STRIP), 0)
    col = lax.broadcasted_iota(jnp.int32, (STRIP, STRIP), 1)
    scale = 1.0 / diag_row_ref[...]
    for source, out, scaled in ((u_ref, u_out, True), (l_ref, l_out, False)):

        def entries(rows, cols):
            return source[rows, cols] * scale[:, cols] if scaled else source[rows, cols]

        strips = [slice(at, at + STRIP) for at in range(0, size, STRIP)]
        strict = [jnp.where(row > col, entries(s, s), 0.0) for s in strips]
        for s, inverse in zip(strips, unit_inverses(strict, STRIP)):
            out[s, s] = inverse
        block = STRIP
        while block < size:
            for at in range(0, size, 2 * block):
                low, high = slice(at, at + block), slice(at + block, at + 2 * block)
                moved = times(split(entries(high, low)), split(out[low, low]))
                out[high, low] = -times(split(out[high, high]), split(moved))
                out[low, high] = jnp.zeros((block, block), F32)
            block *= 2
    u_out[...] = u_out[...] * (1.0 / diag_col_ref[...])


def diagonal_inverses(panel, u_panels, l_panels, u_diag):
    size = u_panels.shape[0]
    square = pl.BlockSpec((size, size), lambda i, p: (0, p[0]))
    return pl.pallas_call(
        inverse_kernel,
        grid_spec=pltpu.PrefetchScalarGridSpec(
            num_scalar_prefetch=1,
            grid=(1,),
            in_specs=[
                square,
                square,
                pl.BlockSpec((1, size), lambda i, p: (0, p[0])),
                pl.BlockSpec((size, 1), lambda i, p: (p[0], 0)),
            ],
            out_specs=[pl.BlockSpec((size, size), lambda i, p: (0, 0))] * 2,
        ),
        out_shape=[jax.ShapeDtypeStruct((size, size), F32)] * 2,
        cost_estimate=pl.CostEstimate(
            flops=8 * size**3, bytes_accessed=16 * size**2, transcendentals=0
        ),
        name="diagonal_inverses",
    )(panel[None], u_panels, l_panels, u_diag[None, :], u_diag[:, None])


def product(left, right, left_dim=1):
    return lax.dot_general(
        left,
        right,
        (((left_dim,), (0,)), ((), ())),
        precision=lax.Precision.HIGH,
        preferred_element_type=F32,
    )


def exchange(value, bit, count):
    return lax.ppermute(value, "row", [(i, i ^ (1 << bit)) for i in range(count)])


def part(value, index):
    rows = value.shape[0] // 2
    return lax.dynamic_slice_in_dim(value, index * rows, rows, 0)


def joined(mine, other, index):
    return jnp.concatenate(
        [jnp.where(index == 0, mine, other), jnp.where(index == 0, other, mine)], axis=0
    )


def along_line(line, me, root, count):
    for bit in range(1, count.bit_length() - 1):
        line = jnp.where((me ^ root) >> bit == 0, line, exchange(line, bit, count))
    return line


def spread(own, me, root, count):
    side = me & 1
    line = jnp.where(me == root, part(own, side), exchange(part(own, 1 - side), 0, count))
    line = along_line(line, me, root, count)
    return joined(line, exchange(line, 0, count), side)


def summed(value, me, count):
    bits = range(count.bit_length() - 1)
    for bit in bits:
        side = me >> bit & 1
        value = part(value, side) + exchange(part(value, 1 - side), bit, count)
    for bit in reversed(bits):
        value = joined(value, exchange(value, bit, count), me >> bit & 1)
    return value


def spread_factors(own, me, roots, count, core, cores):
    size = own.shape[0] // cores
    own = lax.dynamic_slice_in_dim(own, core * size, size, 0)
    side = me & 1
    kept, came = part(own, side), exchange(part(own, 1 - side), 0, count)
    lines = []
    for m in range(1, PANELS):
        cols = slice(0, m * PANEL)
        lines.append(jnp.where(me == roots[m], kept[:, cols], came[:, cols]))
    for bit in range(1, count.bit_length() - 1):
        moved = exchange(jnp.concatenate(lines, axis=1), bit, count)
        at = 0
        for m in range(1, PANELS):
            has = (me ^ roots[m]) >> bit == 0
            lines[m - 1] = jnp.where(has, lines[m - 1], moved[:, at : at + m * PANEL])
            at += m * PANEL
    line = jnp.concatenate(lines, axis=1)
    block = joined(line, exchange(line, 0, count), side)
    pieces = [block]
    for shift in range(1, cores):
        pairs = [(i, (i + shift) % cores) for i in range(cores)]
        pieces.append(lax.ppermute(block, "rhs", pairs))
    stacked = jnp.stack(pieces)
    whole = jnp.concatenate([stacked[(core - c) % cores] for c in range(cores)], axis=0)
    found, at = {}, 0
    for m in range(1, PANELS):
        for k in range(m):
            found[m, k] = whole[:, at : at + PANEL]
            at += PANEL
    return found


def body(count, cores, u_panels, u_diag, l_panels, right_side, x_tail, slot_blocks):
    assert u_panels.shape[0] == PANEL and count & (count - 1) == 0
    me = lax.axis_index("row")
    core = lax.axis_index("rhs")
    mine = slot_blocks[me]
    roots = [jnp.argmax(slot_blocks == k).astype(jnp.int32) for k in range(PANELS)]
    panel = jnp.minimum(mine, PANELS - 1)

    tail = jnp.where(mine >= PANELS, x_tail, 0.0)
    coupled = summed(product(l_panels, tail, 0), me, count)
    u_inverse, l_inverse = diagonal_inverses(panel, u_panels, l_panels, u_diag)

    width = right_side.shape[1] // CHUNKS
    states = [right_side[:, h * width : (h + 1) * width] for h in range(CHUNKS)]
    heads = []
    for k in range(PANELS):
        column = u_panels[:, k * PANEL : (k + 1) * PANEL]
        pieces = []
        for h in range(CHUNKS):
            value = spread(product(u_inverse, states[h]), me, roots[k], count)
            update = states[h] - product(column, value)
            states[h] = jnp.where(mine > k, update, jnp.where(mine == k, value, states[h]))
            pieces.append(value)
        heads.append(jnp.concatenate(pieces, axis=1))
    forward_out = jnp.concatenate(states, axis=1)

    factor = product(l_inverse, l_panels[:, : (PANELS - 1) * PANEL])
    factors = spread_factors(factor, me, roots, count, core, cores)
    reduced = [None] * PANELS
    for k in reversed(range(PANELS)):
        value = heads[k] - coupled[k * PANEL : (k + 1) * PANEL]
        for m in range(k + 1, PANELS):
            value = value - product(factors[m, k], reduced[m], 0)
        reduced[k] = value
    picked = reduced[PANELS - 1]
    for k in range(PANELS - 1):
        picked = jnp.where(mine == k, reduced[k], picked)
    solution_out = jnp.where(mine < PANELS, product(l_inverse, picked, 0), x_tail)
    return forward_out, solution_out


def solution(mesh):
    rows = P(("group", "row"), None)
    both = P(("group", "row"), "rhs")
    return jax.shard_map(
        functools.partial(body, mesh.shape["row"], mesh.shape["rhs"]),
        mesh=mesh,
        in_specs=(rows, P("group"), rows, both, both, P("group")),
        out_specs=(both, both),
        check_vma=False,
    )
```

```python
import functools

import jax
import jax.numpy as jnp
from jax import lax
from jax.experimental import pallas as pl
from jax.experimental.pallas import tpu as pltpu
from jax.sharding import PartitionSpec as P


PANEL = 512
PANELS = 3
CHUNKS = 2
BASE = 8
STRIP = 128
F32 = jnp.float32
BF16 = jnp.bfloat16


def split(value):
    high = value.astype(BF16)
    return high, (value - high.astype(F32)).astype(BF16)


def single(left, right):
    return jnp.dot(left, right, preferred_element_type=F32)


def times(left, right):
    return single(left[0], right[0]) + (single(left[0], right[1]) + single(left[1], right[0]))


def unit_inverses(strict, size):
    row = lax.broadcasted_iota(jnp.int32, (size, size), 0)
    col = lax.broadcasted_iota(jnp.int32, (size, size), 1)
    eye = jnp.where(row == col, 1.0, 0.0)
    powers = [jnp.where(row // BASE == col // BASE, -m, 0.0) for m in strict]
    inverses = [eye + p for p in powers]
    reach = 2
    while reach < BASE:
        halves = [split(p) for p in powers]
        powers = [times(h, h) for h in halves]
        inverses = [x + times(split(p), split(x)) for x, p in zip(inverses, powers)]
        reach *= 2
    block = BASE
    while block < size:
        pair = (row // (2 * block) == col // (2 * block)) & (row // block > col // block)
        between = [split(jnp.where(pair, m, 0.0)) for m in strict]
        halves = [split(x) for x in inverses]
        moved = [times(o, h) for o, h in zip(between, halves)]
        inverses = [x - times(h, split(t)) for x, h, t in zip(inverses, halves, moved)]
        block *= 2
    return inverses


def inverse_kernel(panel_ref, u_ref, l_ref, diag_ref, u_out, l_out):
    size = u_ref.shape[0]
    strips = [slice(at, at + STRIP) for at in range(0, size, STRIP)]
    row = lax.broadcasted_iota(jnp.int32, (STRIP, STRIP), 0)
    col = lax.broadcasted_iota(jnp.int32, (STRIP, STRIP), 1)
    first = panel_ref[0] * len(strips)
    scales = [1.0 / diag_ref[pl.ds(first + i, 1), :] for i in range(len(strips))]
    for source, out, scaled in ((u_ref, u_out, True), (l_ref, l_out, False)):

        def entries(rows, cols):
            if not scaled:
                return source[rows, cols]
            parts = scales[cols.start // STRIP : cols.stop // STRIP]
            return source[rows, cols] * jnp.concatenate(parts, axis=1)

        strict = [jnp.where(row > col, entries(s, s), 0.0) for s in strips]
        for s, inverse in zip(strips, unit_inverses(strict, STRIP)):
            out[s, s] = inverse
        block = STRIP
        while block < size:
            for at in range(0, size, 2 * block):
                low, high = slice(at, at + block), slice(at + block, at + 2 * block)
                moved = times(split(entries(high, low)), split(out[low, low]))
                out[high, low] = -times(split(out[high, high]), split(moved))
                out[low, high] = jnp.zeros((block, block), F32)
            block *= 2
    for s, scale in zip(strips, scales):
        tall = jnp.transpose(jnp.broadcast_to(scale, (STRIP, STRIP)))
        u_out[s, :] = u_out[s, :] * jnp.concatenate([tall] * len(strips), axis=1)


def diagonal_inverses(panel, u_panels, l_panels, u_diag):
    size = u_panels.shape[0]
    diag = u_diag.reshape(-1, STRIP)
    square = pl.BlockSpec((size, size), lambda i, p: (0, p[0]))
    return pl.pallas_call(
        inverse_kernel,
        grid_spec=pltpu.PrefetchScalarGridSpec(
            num_scalar_prefetch=1,
            grid=(1,),
            in_specs=[square, square, pl.BlockSpec(diag.shape, lambda i, p: (0, 0))],
            out_specs=[pl.BlockSpec((size, size), lambda i, p: (0, 0))] * 2,
        ),
        out_shape=[jax.ShapeDtypeStruct((size, size), F32)] * 2,
        cost_estimate=pl.CostEstimate(
            flops=8 * size**3, bytes_accessed=16 * size**2, transcendentals=0
        ),
        name="diagonal_inverses",
    )(panel[None], u_panels, l_panels, diag)


def product(left, right, left_dim=1):
    return lax.dot_general(
        left,
        right,
        (((left_dim,), (0,)), ((), ())),
        precision=lax.Precision.HIGH,
        preferred_element_type=F32,
    )


def exchange(value, bit, count):
    return lax.ppermute(value, "row", [(i, i ^ (1 << bit)) for i in range(count)])


def part(value, index):
    rows = value.shape[0] // 2
    return lax.dynamic_slice_in_dim(value, index * rows, rows, 0)


def joined(mine, other, index):
    return jnp.concatenate(
        [jnp.where(index == 0, mine, other), jnp.where(index == 0, other, mine)], axis=0
    )


def spread(own, me, root, count):
    side = me & 1
    came = exchange(part(own, 1 - side), 0, count)
    line = jnp.where(me == root, part(own, side), came)
    for bit in range(1, count.bit_length() - 1):
        came = exchange(line, bit, count)
        line = jnp.where((me ^ root) >> bit == 0, line, came)
    return joined(line, exchange(line, 0, count), side)


def summed(value, me, count, bits):
    for bit in bits:
        side = me >> bit & 1
        came = exchange(part(value, 1 - side), bit, count)
        value = part(value, side) + came
    for bit in reversed(bits):
        came = exchange(value, bit, count)
        value = joined(value, came, me >> bit & 1)
    return value


def over_cores(block, core, cores):
    pieces = [block]
    for shift in range(1, cores):
        pairs = [(i, (i + shift) % cores) for i in range(cores)]
        pieces.append(lax.ppermute(block, "rhs", pairs))
    stacked = jnp.stack(pieces)
    return jnp.concatenate([stacked[(core - c) % cores] for c in range(cores)], axis=0)


def select_panel(mine, values):
    picked = values[-1]
    for k in range(len(values) - 1):
        picked = jnp.where(mine == k, values[k], picked)
    return picked


def columns(value, k, count=1):
    return value[:, k * PANEL : (k + count) * PANEL]


def rows_of(value, k):
    return value[k * PANEL : (k + 1) * PANEL]


def body(count, cores, u_panels, u_diag, l_panels, right_side, x_tail, slot_blocks):
    assert u_panels.shape[0] == PANEL and count & (count - 1) == 0
    return sweeps(count, cores, u_panels, u_diag, l_panels, right_side, x_tail, slot_blocks)


def sweeps(count, cores, u_panels, u_diag, l_panels, right_side, x_tail, slot_blocks):
    me = lax.axis_index("row")
    core = lax.axis_index("rhs")
    mine = slot_blocks[me]
    roots = [jnp.argmax(slot_blocks == k).astype(jnp.int32) for k in range(PANELS)]
    last = PANELS - 1
    width = right_side.shape[1] // CHUNKS
    chunks = range(CHUNKS)

    def chunked(value):
        return [value[:, h * width : (h + 1) * width] for h in chunks]

    bits = list(range(count.bit_length() - 1))
    orders = [bits, bits[1:2] + bits[:1] + bits[2:]]
    partial = product(l_panels, jnp.where(mine >= PANELS, x_tail, 0.0), 0)
    coupled = [
        summed(piece, me, count, orders[h % 2]) for h, piece in enumerate(chunked(partial))
    ]
    u_inverse, l_inverse = diagonal_inverses(
        jnp.minimum(mine, last), u_panels, l_panels, u_diag
    )

    states = chunked(right_side)
    heads = []

    def update(k, h, value):
        newer = states[h] - product(columns(u_panels, k), value)
        states[h] = jnp.where(mine > k, newer, jnp.where(mine == k, value, states[h]))

    for k in range(last):
        heads.append([])
        for h in chunks:
            value = product(u_inverse, states[h])
            heads[k].append(spread(value, me, roots[k], count))
            update(k, h, heads[k][h])

    factor = product(l_inverse, columns(l_panels, 0, last))
    own = [product(u_inverse, states[h]) for h in chunks]
    lowest = [own[h] - rows_of(coupled[h], last) for h in chunks]
    taken = {}
    for h in chunks:
        for k in reversed(range(last)):
            value = product(columns(factor, k), lowest[h], 0)
            taken[k, h] = spread(value, me, roots[last], count)
    for h in chunks:
        update(last, h, spread(own[h], me, roots[last], count))
    forward_out = jnp.concatenate(states, axis=1)

    size = PANEL // cores
    between = {}
    for m in range(1, last):
        block = lax.dynamic_slice(factor, (core * size, 0), (size, m * PANEL))
        block = over_cores(spread(block, me, roots[m], count), core, cores)
        for k in range(m):
            between[m, k] = columns(block, k)

    pieces = []
    for h in chunks:
        reduced = [None] * last + [lowest[h]]
        for k in reversed(range(last)):
            value = heads[k][h] - rows_of(coupled[h], k) - taken[k, h]
            for m in range(k + 1, last):
                value = value - product(between[m, k], reduced[m], 0)
            reduced[k] = value
        pieces.append(product(l_inverse, select_panel(mine, reduced), 0))
    solved = jnp.concatenate(pieces, axis=1)
    return forward_out, jnp.where(mine < PANELS, solved, x_tail)


def solution(mesh):
    rows = P(("group", "row"), None)
    both = P(("group", "row"), "rhs")
    return jax.shard_map(
        functools.partial(body, mesh.shape["row"], mesh.shape["rhs"]),
        mesh=mesh,
        in_specs=(rows, P("group"), rows, both, both, P("group")),
        out_specs=(both, both),
        check_vma=False,
    )
```

```python
import functools

import jax
import jax.numpy as jnp
from jax import lax
from jax.experimental import pallas as pl
from jax.experimental.pallas import tpu as pltpu
from jax.sharding import PartitionSpec as P


PANEL = 512
PANELS = 3
CHUNKS = 2
BASE = 8
STRIP = 128
F32 = jnp.float32
BF16 = jnp.bfloat16


def split(value):
    high = value.astype(BF16)
    return high, (value - high.astype(F32)).astype(BF16)


def single(left, right):
    return jnp.dot(left, right, preferred_element_type=F32)


def times(left, right):
    return single(left[0], right[0]) + (single(left[0], right[1]) + single(left[1], right[0]))


def unit_inverses(strict, size):
    row = lax.broadcasted_iota(jnp.int32, (size, size), 0)
    col = lax.broadcasted_iota(jnp.int32, (size, size), 1)
    eye = jnp.where(row == col, 1.0, 0.0)
    powers = [jnp.where(row // BASE == col // BASE, -m, 0.0) for m in strict]
    inverses = [eye + p for p in powers]
    reach = 2
    while reach < BASE:
        halves = [split(p) for p in powers]
        powers = [times(h, h) for h in halves]
        inverses = [x + times(split(p), split(x)) for x, p in zip(inverses, powers)]
        reach *= 2
    block = BASE
    while block < size:
        pair = (row // (2 * block) == col // (2 * block)) & (row // block > col // block)
        between = [split(jnp.where(pair, m, 0.0)) for m in strict]
        halves = [split(x) for x in inverses]
        moved = [times(o, h) for o, h in zip(between, halves)]
        inverses = [x - times(h, split(t)) for x, h, t in zip(inverses, halves, moved)]
        block *= 2
    return inverses


def inverse_kernel(panel_ref, u_ref, l_ref, diag_ref, u_out, l_out):
    size = u_ref.shape[0]
    strips = [slice(at, at + STRIP) for at in range(0, size, STRIP)]
    row = lax.broadcasted_iota(jnp.int32, (STRIP, STRIP), 0)
    col = lax.broadcasted_iota(jnp.int32, (STRIP, STRIP), 1)
    first = panel_ref[0] * len(strips)
    scales = [1.0 / diag_ref[pl.ds(first + i, 1), :] for i in range(len(strips))]
    for source, out, scaled in ((u_ref, u_out, True), (l_ref, l_out, False)):

        def entries(rows, cols):
            if not scaled:
                return source[rows, cols]
            parts = scales[cols.start // STRIP : cols.stop // STRIP]
            return source[rows, cols] * jnp.concatenate(parts, axis=1)

        strict = [jnp.where(row > col, entries(s, s), 0.0) for s in strips]
        for s, inverse in zip(strips, unit_inverses(strict, STRIP)):
            out[s, s] = inverse
        block = STRIP
        while block < size:
            for at in range(0, size, 2 * block):
                low, high = slice(at, at + block), slice(at + block, at + 2 * block)
                moved = times(split(entries(high, low)), split(out[low, low]))
                out[high, low] = -times(split(out[high, high]), split(moved))
                out[low, high] = jnp.zeros((block, block), F32)
            block *= 2
    for s, scale in zip(strips, scales):
        tall = jnp.transpose(jnp.broadcast_to(scale, (STRIP, STRIP)))
        u_out[s, :] = u_out[s, :] * jnp.concatenate([tall] * len(strips), axis=1)


def diagonal_inverses(panel, u_panels, l_panels, u_diag):
    size = u_panels.shape[0]
    diag = u_diag.reshape(-1, STRIP)
    square = pl.BlockSpec((size, size), lambda i, p: (0, p[0]))
    return pl.pallas_call(
        inverse_kernel,
        grid_spec=pltpu.PrefetchScalarGridSpec(
            num_scalar_prefetch=1,
            grid=(1,),
            in_specs=[square, square, pl.BlockSpec(diag.shape, lambda i, p: (0, 0))],
            out_specs=[pl.BlockSpec((size, size), lambda i, p: (0, 0))] * 2,
        ),
        out_shape=[jax.ShapeDtypeStruct((size, size), F32)] * 2,
        cost_estimate=pl.CostEstimate(
            flops=8 * size**3, bytes_accessed=16 * size**2, transcendentals=0
        ),
        name="diagonal_inverses",
    )(panel, u_panels, l_panels, diag)


def product(left, right, left_dim=1):
    return lax.dot_general(
        left,
        right,
        (((left_dim,), (0,)), ((), ())),
        precision=lax.Precision.HIGH,
        preferred_element_type=F32,
    )


def places(slot_blocks, width):
    count = slot_blocks.shape[0]
    me, core = lax.axis_index("row"), lax.axis_index("rhs")
    shape = (PANELS + 3, count)
    kind = lax.broadcasted_iota(jnp.int32, shape, 0)
    slot = lax.broadcasted_iota(jnp.int32, shape, 1)
    block = slot_blocks[None, :]
    here = slot == me
    found = jnp.where(kind < PANELS, jnp.where(block == kind, slot, 0), 0)
    found = jnp.where((kind == PANELS) & here, block, found)
    found = jnp.where((kind == PANELS + 1) & here, slot, found)
    found = jnp.where((kind == PANELS + 2) & here, core, found)
    return jnp.broadcast_to(jnp.sum(found, axis=1, keepdims=True), (PANELS + 3, width))


class Places:
    def __init__(self, table):
        self.table = table

    def row(self, at, width):
        return self.table[at : at + 1, :width]

    def root(self, k, width):
        return self.row(k, width)

    def mine(self, width):
        return self.row(PANELS, width)

    def me(self, width):
        return self.row(PANELS + 1, width)

    def core(self, width):
        return self.row(PANELS + 2, width)


def low(index, bit):
    return ((index >> bit) & 1) == 0


def exchange(value, bit, count, axis="row"):
    return lax.ppermute(value, axis, [(i, i ^ (1 << bit)) for i in range(count)])


def part(value, first):
    rows = value.shape[0] // 2
    return jnp.where(first, value[:rows], value[rows:])


def joined(mine, other, first):
    return jnp.concatenate([jnp.where(first, mine, other), jnp.where(first, other, mine)], axis=0)


def spread(own, at, k, count):
    width = own.shape[1]
    me, apart = at.me(width), at.me(width) ^ at.root(k, width)
    first = low(me, 0)
    came = exchange(part(own, ~first), 0, count)
    line = jnp.where(apart == 0, part(own, first), came)
    for bit in range(1, count.bit_length() - 1):
        came = exchange(line, bit, count)
        line = jnp.where(apart >> bit == 0, line, came)
    return joined(line, exchange(line, 0, count), first)


def summed(value, at, count, bits):
    me = at.me(value.shape[1])
    for bit in bits:
        first = low(me, bit)
        came = exchange(part(value, ~first), bit, count)
        value = part(value, first) + came
    for bit in reversed(bits):
        came = exchange(value, bit, count)
        value = joined(value, came, low(me, bit))
    return value


def over_cores(block, at, cores):
    core = at.core(block.shape[1])
    for bit in range(cores.bit_length() - 1):
        block = joined(block, exchange(block, bit, cores, "rhs"), low(core, bit))
    return block


def select_panel(mine, values):
    picked = values[-1]
    for k in range(len(values) - 1):
        picked = jnp.where(mine == k, values[k], picked)
    return picked


def columns(value, k, count=1):
    return value[:, k * PANEL : (k + count) * PANEL]


def rows_of(value, k):
    return value[k * PANEL : (k + 1) * PANEL]


def body(count, cores, *args):
    assert args[0].shape[0] == PANEL and count & (count - 1) == 0 and cores & (cores - 1) == 0
    return sweeps(count, cores, *args)


def sweeps(count, cores, u_panels, u_diag, l_panels, right_side, x_tail, slot_blocks):
    last = PANELS - 1
    whole = right_side.shape[1]
    width = whole // CHUNKS
    chunks = range(CHUNKS)
    at = Places(places(slot_blocks, PANEL))
    mine = at.mine(width)

    def chunked(value):
        return [value[:, h * width : (h + 1) * width] for h in chunks]

    u_inverse, l_inverse = diagonal_inverses(
        jnp.minimum(at.table[PANELS, :1], last), u_panels, l_panels, u_diag
    )
    bits = list(range(count.bit_length() - 1))
    orders = [bits, bits[1:2] + bits[:1] + bits[2:]]
    partial = product(l_panels, jnp.where(at.mine(whole) >= PANELS, x_tail, 0.0), 0)
    coupled = [summed(piece, at, count, orders[h % 2]) for h, piece in enumerate(chunked(partial))]

    states = chunked(right_side)
    heads = []

    def update(k, h, value):
        newer = states[h] - product(columns(u_panels, k), value)
        states[h] = jnp.where(mine > k, newer, jnp.where(mine == k, value, states[h]))

    for k in range(last):
        heads.append([])
        for h in chunks:
            value = product(u_inverse, states[h])
            heads[k].append(spread(value, at, k, count))
            update(k, h, heads[k][h])

    factor = product(l_inverse, columns(l_panels, 0, last))
    own = [product(u_inverse, states[h]) for h in chunks]
    lowest = [own[h] - rows_of(coupled[h], last) for h in chunks]
    taken = [spread(product(factor, lowest[h], 0), at, last, count) for h in chunks]
    for h in chunks:
        update(last, h, spread(own[h], at, last, count))
    forward_out = jnp.concatenate(states, axis=1)

    between = {}
    for m in range(1, last):
        block = columns(factor, 0, m)
        for bit in reversed(range(cores.bit_length() - 1)):
            block = part(block, low(at.core(m * PANEL), bit))
        block = over_cores(spread(block, at, m, count), at, cores)
        for k in range(m):
            between[m, k] = columns(block, k)

    pieces = []
    for h in chunks:
        reduced = [None] * last + [lowest[h]]
        for k in reversed(range(last)):
            value = heads[k][h] - rows_of(coupled[h], k) - rows_of(taken[h], k)
            for m in range(k + 1, last):
                value = value - product(between[m, k], reduced[m], 0)
            reduced[k] = value
        pieces.append(product(l_inverse, select_panel(mine, reduced), 0))
    solved = jnp.concatenate(pieces, axis=1)
    return forward_out, jnp.where(at.mine(whole) < PANELS, solved, x_tail)


def solution(mesh):
    rows = P(("group", "row"), None)
    both = P(("group", "row"), "rhs")
    return jax.shard_map(
        functools.partial(body, mesh.shape["row"], mesh.shape["rhs"]),
        mesh=mesh,
        in_specs=(rows, P("group"), rows, both, both, P("group")),
        out_specs=(both, both),
        check_vma=False,
    )
```

```python
import functools

import jax
import jax.numpy as jnp
from jax import lax
from jax.experimental import pallas as pl
from jax.experimental.pallas import tpu as pltpu
from jax.sharding import PartitionSpec as P


PANEL = 512
PANELS = 3
CHUNKS = 2
BASE = 8
STRIP = 128
F32 = jnp.float32
BF16 = jnp.bfloat16


def split(value):
    high = value.astype(BF16)
    return high, (value - high.astype(F32)).astype(BF16)


def single(left, right):
    return jnp.dot(left, right, preferred_element_type=F32)


def times(left, right):
    return single(left[0], right[0]) + (single(left[0], right[1]) + single(left[1], right[0]))


def unit_inverses(strict, size):
    row = lax.broadcasted_iota(jnp.int32, (size, size), 0)
    col = lax.broadcasted_iota(jnp.int32, (size, size), 1)
    eye = jnp.where(row == col, 1.0, 0.0)
    powers = [jnp.where(row // BASE == col // BASE, -m, 0.0) for m in strict]
    inverses = [eye + p for p in powers]
    reach = 2
    while reach < BASE:
        halves = [split(p) for p in powers]
        powers = [times(h, h) for h in halves]
        inverses = [x + times(split(p), split(x)) for x, p in zip(inverses, powers)]
        reach *= 2
    block = BASE
    while block < size:
        pair = (row // (2 * block) == col // (2 * block)) & (row // block > col // block)
        between = [split(jnp.where(pair, m, 0.0)) for m in strict]
        halves = [split(x) for x in inverses]
        moved = [times(o, h) for o, h in zip(between, halves)]
        inverses = [x - times(h, split(t)) for x, h, t in zip(inverses, halves, moved)]
        block *= 2
    return inverses


def decisions(count, cores):
    bits = range(count.bit_length() - 1)
    found = {}
    for k in range(PANELS):
        for bit in bits:
            found["has", k, bit] = lambda me, core, mine, roots, k=k, bit=bit: (
                (me ^ roots[k]) >> bit == 0
            )
        found["is", k] = lambda me, core, mine, roots, k=k: mine == k
        found["past", k] = lambda me, core, mine, roots, k=k: mine > k
    for bit in bits:
        found["low", bit] = lambda me, core, mine, roots, bit=bit: (me >> bit) & 1 == 0
    for bit in range(cores.bit_length() - 1):
        found["core", bit] = lambda me, core, mine, roots, bit=bit: (core >> bit) & 1 == 0
    return found


def inverse_kernel(
    tests, blocks_ref, me_ref, core_ref, u_ref, l_ref, diag_ref, u_out, l_out, lt_out, flags_out
):
    size = u_ref.shape[0]
    me, core = me_ref[0], core_ref[0]
    mine = blocks_ref[me]
    roots = [jnp.int32(0)] * PANELS
    for slot in range(blocks_ref.shape[0]):
        block = blocks_ref[slot]
        roots = [jnp.where(block == k, slot, root) for k, root in enumerate(roots)]
    for at, test in enumerate(tests):
        flag = jnp.where(test(me, core, mine, roots), 1, 0)
        flags_out[at : at + 1, :] = jnp.full((1, size), flag, jnp.int32)
    panel = jnp.minimum(mine, PANELS - 1)
    strips = [slice(at, at + STRIP) for at in range(0, size, STRIP)]
    row = lax.broadcasted_iota(jnp.int32, (STRIP, STRIP), 0)
    col = lax.broadcasted_iota(jnp.int32, (STRIP, STRIP), 1)
    first = panel * len(strips)
    scales = [1.0 / diag_ref[pl.ds(first + i, 1), :] for i in range(len(strips))]
    for source, out, scaled in ((u_ref, u_out, True), (l_ref, l_out, False)):

        def entries(rows, cols):
            if not scaled:
                return source[rows, cols]
            parts = scales[cols.start // STRIP : cols.stop // STRIP]
            return source[rows, cols] * jnp.concatenate(parts, axis=1)

        strict = [jnp.where(row > col, entries(s, s), 0.0) for s in strips]
        for s, inverse in zip(strips, unit_inverses(strict, STRIP)):
            out[s, s] = inverse
        block = STRIP
        while block < size:
            for at in range(0, size, 2 * block):
                low, high = slice(at, at + block), slice(at + block, at + 2 * block)
                moved = times(split(entries(high, low)), split(out[low, low]))
                out[high, low] = -times(split(out[high, high]), split(moved))
                out[low, high] = jnp.zeros((block, block), F32)
            block *= 2
    for s, scale in zip(strips, scales):
        tall = jnp.transpose(jnp.broadcast_to(scale, (STRIP, STRIP)))
        u_out[s, :] = u_out[s, :] * jnp.concatenate([tall] * len(strips), axis=1)
    for i in strips:
        for j in strips:
            lt_out[j, i] = jnp.transpose(l_out[i, j])


def diagonal_inverses(blocks, u_panels, l_panels, u_diag, cores):
    size = u_panels.shape[0]
    tests = list(decisions(blocks.shape[0], cores).values())
    diag = u_diag.reshape(-1, STRIP)
    own = pl.BlockSpec((size, size), lambda i, b, me, core: (0, jnp.minimum(b[me[0]], PANELS - 1)))
    square = pl.BlockSpec((size, size), lambda i, *refs: (0, 0))
    flags = (len(tests), size)
    return pl.pallas_call(
        functools.partial(inverse_kernel, tests),
        grid_spec=pltpu.PrefetchScalarGridSpec(
            num_scalar_prefetch=3,
            grid=(1,),
            in_specs=[own, own, pl.BlockSpec(diag.shape, lambda i, *refs: (0, 0))],
            out_specs=[square] * 3 + [pl.BlockSpec(flags, lambda i, *refs: (0, 0))],
        ),
        out_shape=[jax.ShapeDtypeStruct((size, size), F32)] * 3
        + [jax.ShapeDtypeStruct(flags, jnp.int32)],
        cost_estimate=pl.CostEstimate(
            flops=8 * size**3, bytes_accessed=20 * size**2, transcendentals=0
        ),
        name="diagonal_inverses",
    )(blocks, lax.axis_index("row")[None], lax.axis_index("rhs")[None], u_panels, l_panels, diag)


def finish_kernel(row, table_ref, inverse_ref, tail_ref, *refs):
    chunks, out = refs[:-1], refs[-1]
    width = chunks[0].shape[1]
    inverse = split(inverse_ref[...])
    keep = table_ref[row : row + 1, :width] != 0
    for h, chunk in enumerate(chunks):
        at = slice(h * width, (h + 1) * width)
        out[:, at] = jnp.where(keep, tail_ref[:, at], times(inverse, split(chunk[...])))


def finished(row, table, inverse, tail, chunks):
    return pl.pallas_call(
        functools.partial(finish_kernel, row),
        out_shape=jax.ShapeDtypeStruct(tail.shape, F32),
        cost_estimate=pl.CostEstimate(
            flops=6 * inverse.size * tail.shape[1], bytes_accessed=4 * inverse.size, transcendentals=0
        ),
        name="finished",
    )(table, inverse, tail, *chunks)


def product(left, right, left_dim=1):
    return lax.dot_general(
        left,
        right,
        (((left_dim,), (0,)), ((), ())),
        precision=lax.Precision.HIGH,
        preferred_element_type=F32,
    )


class Places:
    def __init__(self, table, count, cores):
        self.table = table
        self.rows = {name: row for row, name in enumerate(decisions(count, cores))}

    def pick(self, name, left, right):
        row = self.rows[name]
        return jnp.where(self.table[row : row + 1, : left.shape[1]] != 0, left, right)


def exchange(value, bit, count, axis="row"):
    return lax.ppermute(value, axis, [(i, i ^ (1 << bit)) for i in range(count)])


def parts(value, at, name):
    rows = value.shape[0] // 2
    top, bottom = value[:rows], value[rows:]
    return at.pick(name, top, bottom), at.pick(name, bottom, top)


def joined(mine, other, at, name):
    return jnp.concatenate([at.pick(name, mine, other), at.pick(name, other, mine)], axis=0)


def spread(own, at, k, count):
    kept, sent = parts(own, at, ("low", 0))
    came = exchange(sent, 0, count)
    line = at.pick(("has", k, 0), kept, came)
    for bit in range(1, count.bit_length() - 1):
        came = exchange(line, bit, count)
        line = at.pick(("has", k, bit), line, came)
    return joined(line, exchange(line, 0, count), at, ("low", 0))


def summed(value, at, count, bits):
    for bit in bits:
        kept, sent = parts(value, at, ("low", bit))
        value = kept + exchange(sent, bit, count)
    for bit in reversed(bits):
        value = joined(value, exchange(value, bit, count), at, ("low", bit))
    return value


def over_cores(block, at, cores):
    for bit in range(cores.bit_length() - 1):
        block = joined(block, exchange(block, bit, cores, "rhs"), at, ("core", bit))
    return block


def columns(value, k, count=1):
    return value[:, k * PANEL : (k + count) * PANEL]


def rows_of(value, k):
    return value[k * PANEL : (k + 1) * PANEL]


def body(count, cores, *args):
    assert args[0].shape[0] == PANEL and count & (count - 1) == 0 and cores & (cores - 1) == 0
    return sweeps(count, cores, *args)


def sweeps(count, cores, u_panels, u_diag, l_panels, right_side, x_tail, slot_blocks):
    last = PANELS - 1
    whole = right_side.shape[1]
    width = whole // CHUNKS
    chunks = range(CHUNKS)

    def chunked(value):
        return [value[:, h * width : (h + 1) * width] for h in chunks]

    u_inverse, _, l_inverse_t, table = diagonal_inverses(
        slot_blocks, u_panels, l_panels, u_diag, cores
    )
    at = Places(table, count, cores)
    bits = list(range(count.bit_length() - 1))
    orders = [bits, bits[1:2] + bits[:1] + bits[2:]]
    partial = product(l_panels, at.pick(("past", last), x_tail, jnp.zeros_like(x_tail)), 0)
    coupled = [summed(piece, at, count, orders[h % 2]) for h, piece in enumerate(chunked(partial))]

    states = chunked(right_side)
    heads = []

    def update(k, h, value):
        newer = states[h] - product(columns(u_panels, k), value)
        newer = at.pick(("past", k), newer, states[h])
        states[h] = at.pick(("is", k), value, newer)

    for k in range(last):
        heads.append([])
        for h in chunks:
            value = product(u_inverse, states[h])
            heads[k].append(spread(value, at, k, count))
            update(k, h, heads[k][h])

    factor = product(columns(l_panels, 0, last), l_inverse_t, 0)
    own = [product(u_inverse, states[h]) for h in chunks]
    lowest = [own[h] - rows_of(coupled[h], last) for h in chunks]
    taken = {}
    for h in chunks:
        update(last, h, spread(own[h], at, last, count))
    for h in chunks:
        for k in reversed(range(last)):
            value = product(rows_of(factor, k), lowest[h])
            taken[k, h] = spread(value, at, last, count)
    forward_out = jnp.concatenate(states, axis=1)

    between = {}
    for m in range(1, last):
        block = factor[: m * PANEL]
        for bit in reversed(range(cores.bit_length() - 1)):
            block = parts(block, at, ("core", bit))[0]
        block = over_cores(spread(block, at, m, count), at, cores)
        for k in range(m):
            between[m, k] = rows_of(block, k)

    pieces = []
    for h in chunks:
        reduced = [None] * last + [lowest[h]]
        for k in reversed(range(last)):
            value = heads[k][h] - rows_of(coupled[h], k) - taken[k, h]
            for m in range(k + 1, last):
                value = value - product(between[m, k], reduced[m])
            reduced[k] = value
        picked = reduced[last]
        for k in range(last):
            picked = at.pick(("is", k), reduced[k], picked)
        pieces.append(picked)
    row = at.rows["past", last]
    return forward_out, finished(row, table, l_inverse_t, x_tail, pieces)


def solution(mesh):
    rows = P(("group", "row"), None)
    both = P(("group", "row"), "rhs")
    return jax.shard_map(
        functools.partial(body, mesh.shape["row"], mesh.shape["rhs"]),
        mesh=mesh,
        in_specs=(rows, P("group"), rows, both, both, P("group")),
        out_specs=(both, both),
        check_vma=False,
    )
```
